768 devices in a mesh: dp: 16 (over y_lo, x), enode: 12 (over z), echip: 4 (over y_hi, core).
Axes of the slice: x: 4, y: 8 (y_hi: 2, y_lo: 4; y = y_hi * 4 + y_lo), z: 12, core: 2. Of those that a mesh axis runs over, the one named last changes fastest.
Arguments:
- hidden: bfloat16 [4608, 7168], P(('dp', 'enode', 'echip')), may hold values from -6 to 6
- grad_out: bfloat16 [4608, 7168], P(('dp', 'enode', 'echip')), may hold values from -6 to 6
- routes: int32 [16, 12, 4, 6, 2], P('dp', None, 'echip'), may hold values from 0 to 3, as said below
- combine: float32 [16, 12, 4, 6, 2], P('dp', None, 'echip'), may hold values from 0.1 to 0.7
- w_gate: bfloat16 [4, 7168, 1536], P('echip', None, 'enode'), may hold values from -0.0625 to 0.0625
- w_up: bfloat16 [4, 7168, 1536], P('echip', None, 'enode'), may hold values from -0.0625 to 0.0625
- w_down: bfloat16 [4, 1536, 7168], P('echip', 'enode'), may hold values from -0.15625 to 0.15625
Outputs:
- layer_out: bfloat16 [4608, 7168], P(('dp', 'enode', 'echip'))
- grad_in: bfloat16 [4608, 7168], P(('dp', 'enode', 'echip'))
- grad_gate: bfloat16 [4, 7168, 1536], P('echip', 'dp', 'enode')
- grad_up: bfloat16 [4, 7168, 1536], P('echip', 'dp', 'enode')
- grad_down: bfloat16 [4, 1536, 7168], P('echip', 'enode', 'dp')
The draws below stay inside these ranges and needn't reach their ends.
Inputs may be any that keep to these rules, and one draw needn't show every extreme that they name: `routes`: each token names 2 different experts, and the 6 tokens of each device name every expert exactly 6 * 2 / 4 times.
All inputs are finite; a program needn't handle non-finite values.
Results may differ from the reference program's by a relative error of at most 0.015.
Values may be sent and summed in bfloat16 or wider, within the bound.
No kernel may reach another device: no remote copies, remote signals or barrier semaphores. Data moves between devices by JAX's collectives and lax.ppermute only.
A program may use at most 64 MiB of HBM per device.

```python
import jax
import jax.numpy as jnp
from jax import lax

D = 7168
FF_WIN = 1536
TOPK = 2
TOK_DEV = 6
EXPERTS = 4
F_DEV = 128
TOKENS = 4608
N_DP = 16
N_ENODE = 12
N_ECHIP = 4


def draw_routes(key, part):
    device_count = N_DP * N_ENODE * N_ECHIP
    expert_key, token_key = jax.random.split(key)
    expert_orders = jax.vmap(lambda subkey: jax.random.permutation(subkey, EXPERTS))(jax.random.split(expert_key, device_count))
    token_orders = jax.vmap(lambda subkey: jax.random.permutation(subkey, TOK_DEV))(jax.random.split(token_key, device_count))
    pattern = (jnp.arange(TOK_DEV)[:, None] * TOPK + jnp.arange(TOPK)[None, :]) % EXPERTS
    shuffled = pattern[token_orders]
    chosen = jax.vmap(lambda order_row, index_rows: order_row[index_rows])(expert_orders, shuffled)
    return chosen.reshape(N_DP, N_ENODE, N_ECHIP, TOK_DEV, TOPK).astype(jnp.int32)


def block_scale(rng, dims, pieces, smallest, largest):
    gain, own = 1.0, jax.random.fold_in(rng, 6)
    for axis_at, shards_of in pieces:
        steps = jnp.exp(jax.random.uniform(jax.random.fold_in(own, axis_at), (shards_of,), jnp.float32, smallest / len(pieces), largest / len(pieces)))
        gain = gain * jnp.repeat(steps, dims[axis_at] // shards_of).reshape([-1 if axis == axis_at else 1 for axis in range(len(dims))])
    return gain


def centred(own_key, extent, deviation, limit, cuts=(), dtype=jnp.bfloat16):
    array = deviation * jax.random.normal(own_key, extent, jnp.float32)
    if cuts:
        array = array * block_scale(own_key, extent, cuts, -0.22, 0.18)
    return jnp.clip(array, -limit, limit).astype(dtype)


def setup_inputs(seed: int = 0) -> dict:
    seeds = jax.random.split(jax.random.key(seed), 8)
    hidden = centred(seeds[0], (TOKENS, D), 1.0, 6.0, ((0, 768),))
    grad_out = centred(seeds[1], (TOKENS, D), 1.0, 6.0, ((0, 768),))
    routes = draw_routes(jax.random.fold_in(seeds[7], 71), 0)
    combine = jnp.clip(0.1 + 0.59999999 * jax.random.uniform(seeds[3], (N_DP, N_ENODE, N_ECHIP, TOK_DEV, TOPK), jnp.float32) ** block_scale(seeds[3], (N_DP, N_ENODE, N_ECHIP, TOK_DEV, TOPK), ((0, 16), (2, 4)), -0.2, 0.2), 0.1, 0.7)
    w_gate = centred(seeds[4], (EXPERTS, D, FF_WIN), D ** -0.5, 0.0625, ((0, 4), (2, 12)))
    w_up = centred(seeds[5], (EXPERTS, D, FF_WIN), D ** -0.5, 0.0625, ((0, 4), (2, 12)))
    w_down = centred(seeds[6], (EXPERTS, FF_WIN, D), FF_WIN ** -0.5, 0.15625, ((0, 4), (1, 12)))
    return {"hidden": hidden, "grad_out": grad_out, "routes": routes, "combine": combine, "w_gate": w_gate, "w_up": w_up, "w_down": w_down}


def group_total(left, right):
    def add_group(running, operands):
        partial_value = jnp.dot(operands[0].T, operands[1], preferred_element_type=jnp.float32)
        rounded = lax.optimization_barrier(partial_value.astype(jnp.bfloat16))
        return running + rounded.astype(jnp.float32), None

    start_sum = jnp.zeros((left.shape[2], right.shape[2]), jnp.float32)
    summed, unused = lax.scan(add_group, start_sum, (left, right))
    return summed.astype(jnp.bfloat16)


def block_sum(partial_value):
    rounded = lax.optimization_barrier(partial_value.astype(jnp.bfloat16))
    return jnp.sum(rounded.astype(jnp.float32), axis=0)


def reference(hidden, grad_out, routes, combine, w_gate, w_up, w_down):
    flat_ids = routes.reshape(TOKENS * TOPK)
    flat_wts = combine.reshape(TOKENS * TOPK)
    expert_rows = TOKENS * TOPK // EXPERTS
    layer_acc = jnp.zeros((TOKENS, D), jnp.float32)
    grad_acc = jnp.zeros((TOKENS, D), jnp.float32)
    gate_list = []
    up_list = []
    down_list = []
    for expert in range(EXPERTS):
        picked = jnp.nonzero(flat_ids == expert, size=expert_rows)[0].astype(jnp.int32)
        token_ids = (picked // TOPK).astype(jnp.int32)
        row_tokens = hidden[token_ids]
        row_weights = flat_wts[picked]
        cot_rows = (grad_out[token_ids].astype(jnp.float32) * row_weights[:, None]).astype(jnp.bfloat16)
        gate_pre = jnp.dot(row_tokens, w_gate[expert], preferred_element_type=jnp.float32)
        up_pre = jnp.dot(row_tokens, w_up[expert], preferred_element_type=jnp.float32)
        sigmoid_gate = jax.nn.sigmoid(gate_pre)
        hid_rows = (gate_pre * sigmoid_gate * up_pre).astype(jnp.bfloat16)
        hid_blocks = hid_rows.reshape(expert_rows, N_ENODE, F_DEV).astype(jnp.float32)
        down_blocks = w_down[expert].reshape(N_ENODE, F_DEV, D).astype(jnp.float32)
        out_rows = block_sum(jnp.einsum("rnf,nfd->nrd", hid_blocks, down_blocks))
        hidden_grad = jnp.dot(cot_rows, w_down[expert].T, preferred_element_type=jnp.float32)
        dgate_rows = (hidden_grad * up_pre * sigmoid_gate * (1.0 + gate_pre * (1.0 - sigmoid_gate))).astype(jnp.bfloat16)
        dup_rows = (hidden_grad * gate_pre * sigmoid_gate).astype(jnp.bfloat16)
        gate_blocks = w_gate[expert].reshape(D, N_ENODE, F_DEV).astype(jnp.float32)
        up_blocks = w_up[expert].reshape(D, N_ENODE, F_DEV).astype(jnp.float32)
        dgate_blocks = dgate_rows.reshape(expert_rows, N_ENODE, F_DEV).astype(jnp.float32)
        dup_blocks = dup_rows.reshape(expert_rows, N_ENODE, F_DEV).astype(jnp.float32)
        dx_terms = jnp.einsum("rnf,dnf->nrd", dgate_blocks, gate_blocks) + jnp.einsum("rnf,dnf->nrd", dup_blocks, up_blocks)
        dx_rows = block_sum(dx_terms)
        layer_acc = layer_acc.at[token_ids].add(row_weights[:, None] * out_rows)
        grad_acc = grad_acc.at[token_ids].add(dx_rows)
        gate_list.append(group_total(row_tokens.reshape(N_DP, -1, D), dgate_rows.reshape(N_DP, -1, FF_WIN)))
        up_list.append(group_total(row_tokens.reshape(N_DP, -1, D), dup_rows.reshape(N_DP, -1, FF_WIN)))
        down_list.append(group_total(hid_rows.reshape(N_DP, -1, FF_WIN), cot_rows.reshape(N_DP, -1, D)))
    return (layer_acc.astype(jnp.bfloat16), grad_acc.astype(jnp.bfloat16), jnp.stack(gate_list), jnp.stack(up_list), jnp.stack(down_list))
```

```python
import jax
import jax.numpy as jnp
from jax import lax
from jax.sharding import Mesh, PartitionSpec as P


def slot_plan(expert_ids, gate_wts, experts):
    token_count, topk_count = expert_ids.shape
    entry_count = token_count * topk_count
    slots = entry_count // experts
    ids = expert_ids.reshape(entry_count)
    order = jnp.arange(entry_count)
    earlier = (ids[None, :] == ids[:, None]) & (order[None, :] < order[:, None])
    rank = jnp.sum(earlier.astype(jnp.int32), axis=1)
    row_of = ids * (2 * slots) + rank
    rows = jnp.arange(experts * 2 * slots)
    hit_tok = (rows[:, None] == row_of[None, :]).astype(jnp.float32)
    hit_cot = (rows[:, None] == (row_of + slots)[None, :]).astype(jnp.float32)
    wts = gate_wts.reshape(1, entry_count)
    pick_tok = jnp.sum(hit_tok.reshape(-1, token_count, topk_count), axis=2)
    pick_cot = jnp.sum(hit_cot.reshape(-1, token_count, topk_count), axis=2)
    mix_out = jnp.sum((hit_cot * wts).reshape(-1, token_count, topk_count), axis=2)
    cot_weight = jnp.sum(hit_cot * wts, axis=1)
    return pick_tok, pick_cot, mix_out, cot_weight, slots


def local(hidden, grad_out, routes, combine, w_gate, w_up, w_down):
    experts = lax.axis_size("yh") * lax.axis_size("c")
    width = hidden.shape[1]
    f_dev = w_gate.shape[2]
    node = lax.axis_index("z")
    ids = lax.dynamic_index_in_dim(routes[0, :, 0], node, 0, keepdims=False)
    wts = lax.dynamic_index_in_dim(combine[0, :, 0], node, 0, keepdims=False)
    pick_tok, pick_cot, mix_out, cot_weight, slots = slot_plan(ids, wts, experts)
    bf16 = jnp.bfloat16
    weights = jnp.concatenate([w_gate[0], w_up[0], w_down[0].T], axis=1)

    send_tok = jnp.dot(pick_tok.astype(bf16), hidden, preferred_element_type=jnp.float32)
    send_cot = jnp.dot(pick_cot.astype(bf16), grad_out, preferred_element_type=jnp.float32)
    send = (send_tok + send_cot * cot_weight[:, None]).astype(bf16)
    own = send.shape[0]
    got = lax.all_to_all(
        send.reshape(experts, own // experts, width), ("yh", "c"), split_axis=0, concat_axis=0, tiled=True
    ).reshape(own, width)
    rows = lax.all_gather(got, "z", axis=0, tiled=True)

    pre = jnp.dot(rows, weights, preferred_element_type=jnp.float32)
    gate_pre = pre[:, :f_dev]
    up_pre = pre[:, f_dev : 2 * f_dev]
    hidden_grad = jnp.roll(pre[:, 2 * f_dev :], -slots, axis=0)
    is_tok = ((jnp.arange(rows.shape[0]) % (2 * slots)) < slots)[:, None]
    sig = jax.nn.sigmoid(gate_pre)
    hid = gate_pre * sig * up_pre
    dgate = hidden_grad * up_pre * sig * (1.0 + gate_pre * (1.0 - sig))
    dup = hidden_grad * gate_pre * sig
    mids = jnp.concatenate(
        [
            jnp.where(is_tok, dgate, 0.0),
            jnp.where(is_tok, dup, 0.0),
            jnp.where(is_tok, 0.0, jnp.roll(hid, slots, axis=0)),
        ],
        axis=1,
    ).astype(bf16)

    shares = lax.dot_general(
        rows, mids, (((0,), (0,)), ((), ())), preferred_element_type=jnp.float32
    ).astype(bf16)
    parts = lax.dot_general(
        mids, weights, (((1,), (1,)), ((), ())), preferred_element_type=jnp.float32
    ).astype(bf16)
    summed = lax.psum_scatter(parts, "z", scatter_dimension=0, tiled=True)
    grads = lax.psum_scatter(shares, ("yl", "x"), scatter_dimension=0, tiled=True)
    back = lax.all_to_all(
        summed.reshape(experts, own // experts, width), ("yh", "c"), split_axis=0, concat_axis=0, tiled=True
    ).reshape(own, width).astype(jnp.float32)
    high = lax.Precision.HIGHEST
    layer_out = jnp.dot(mix_out.T, back, precision=high).astype(bf16)
    grad_in = jnp.dot(pick_tok.T, back, precision=high).astype(bf16)
    grad_gate = grads[None, :, :f_dev]
    grad_up = grads[None, :, f_dev : 2 * f_dev]
    grad_down = grads[:, 2 * f_dev :].T[None]
    return (layer_out, grad_in, grad_gate, grad_up, grad_down)


def solution(mesh):
    fine = Mesh(mesh.devices.reshape(4, 4, 12, 2, 2), ("yl", "x", "z", "yh", "c"))
    dp, echip = ("yl", "x"), ("yh", "c")
    every = dp + ("z",) + echip
    return jax.shard_map(
        local,
        mesh=fine,
        in_specs=(
            P(every, None),
            P(every, None),
            P(dp, None, echip, None, None),
            P(dp, None, echip, None, None),
            P(echip, None, "z"),
            P(echip, None, "z"),
            P(echip, "z", None),
        ),
        out_specs=(
            P(every, None),
            P(every, None),
            P(echip, dp, "z"),
            P(echip, dp, "z"),
            P(echip, "z", dp),
        ),
        check_vma=False,
    )
```

```python
import jax
import jax.numpy as jnp
from jax import lax
from jax.sharding import Mesh, PartitionSpec as P


def slot_plan(expert_ids, gate_wts, experts):
    token_count, topk_count = expert_ids.shape
    entry_count = token_count * topk_count
    slots = entry_count // experts
    ids = expert_ids.reshape(entry_count)
    order = jnp.arange(entry_count)
    earlier = (ids[None, :] == ids[:, None]) & (order[None, :] < order[:, None])
    rank = jnp.sum(earlier.astype(jnp.int32), axis=1)
    row_of = ids * (2 * slots) + rank
    rows = jnp.arange(experts * 2 * slots)
    hit_tok = (rows[:, None] == row_of[None, :]).astype(jnp.float32)
    hit_cot = (rows[:, None] == (row_of + slots)[None, :]).astype(jnp.float32)
    wts = gate_wts.reshape(1, entry_count)
    pick_tok = jnp.sum(hit_tok.reshape(-1, token_count, topk_count), axis=2)
    pick_cot = jnp.sum(hit_cot.reshape(-1, token_count, topk_count), axis=2)
    mix_out = jnp.sum((hit_cot * wts).reshape(-1, token_count, topk_count), axis=2)
    cot_weight = jnp.sum(hit_cot * wts, axis=1)
    return pick_tok, pick_cot, mix_out, cot_weight, slots


def shift(value, axis, step):
    size = lax.axis_size(axis)
    return lax.ppermute(value, axis, [(i, (i + step) % size) for i in range(size)])


def total(*terms):
    return sum(term.astype(jnp.float32) for term in terms).astype(jnp.bfloat16)


def scatter_shares(shares, pieces):
    nx, ny = lax.axis_size("x"), lax.axis_size("yl")
    px, py = lax.axis_index("x"), lax.axis_index("yl")
    grid = shares.reshape(ny, nx, shares.shape[0] // (nx * ny), shares.shape[1])
    rows = grid.shape[2] // pieces
    low, high = slice(0, ny // 2), slice(ny // 2, ny)
    done = []
    for piece in range(pieces):
        part = grid[:, :, piece * rows : (piece + 1) * rows]

        def chunk(step, half):
            return lax.dynamic_index_in_dim(part[half], (px + step) % nx, 1, keepdims=False)

        far_low = shift(chunk(2, low), "x", 1)
        far_high = shift(chunk(2, high), "x", -1)
        near_high = shift(chunk(1, high), "x", 1)
        near_low = shift(chunk(-1, low), "x", -1)
        rest_low = shift(total(chunk(1, low), far_low), "x", 1)
        rest_high = shift(total(chunk(-1, high), far_high), "x", -1)
        mine = jnp.concatenate(
            [total(chunk(0, low), near_low, rest_low), total(chunk(0, high), near_high, rest_high)], axis=0
        )

        def target(step):
            return lax.dynamic_index_in_dim(mine, (py + step) % ny, 0, keepdims=False)

        done.append(total(target(0), *[shift(target(step), "yl", step) for step in range(1, ny)]))
    return jnp.concatenate(done, axis=0)


def local(hidden, grad_out, routes, combine, w_gate, w_up, w_down):
    experts = lax.axis_size("yh") * lax.axis_size("c")
    width = hidden.shape[1]
    f_dev = w_gate.shape[2]
    node = lax.axis_index("z")
    ids = lax.dynamic_index_in_dim(routes[0, :, 0], node, 0, keepdims=False)
    wts = lax.dynamic_index_in_dim(combine[0, :, 0], node, 0, keepdims=False)
    pick_tok, pick_cot, mix_out, cot_weight, slots = slot_plan(ids, wts, experts)
    bf16 = jnp.bfloat16
    weights = jnp.concatenate([w_gate[0], w_up[0], w_down[0].T], axis=1)

    send_tok = jnp.dot(pick_tok.astype(bf16), hidden, preferred_element_type=jnp.float32)
    send_cot = jnp.dot(pick_cot.astype(bf16), grad_out, preferred_element_type=jnp.float32)
    send = (send_tok + send_cot * cot_weight[:, None]).astype(bf16)
    own = send.shape[0]
    got = lax.all_to_all(
        send.reshape(experts, own // experts, width), ("yh", "c"), split_axis=0, concat_axis=0, tiled=True
    ).reshape(own, width)
    rows = lax.all_gather(got, "z", axis=0, tiled=True)

    pre = jnp.dot(rows, weights, preferred_element_type=jnp.float32)
    gate_pre = pre[:, :f_dev]
    up_pre = pre[:, f_dev : 2 * f_dev]
    hidden_grad = jnp.roll(pre[:, 2 * f_dev :], -slots, axis=0)
    is_tok = ((jnp.arange(rows.shape[0]) % (2 * slots)) < slots)[:, None]
    sig = jax.nn.sigmoid(gate_pre)
    hid = gate_pre * sig * up_pre
    dgate = hidden_grad * up_pre * sig * (1.0 + gate_pre * (1.0 - sig))
    dup = hidden_grad * gate_pre * sig
    mids = jnp.concatenate(
        [
            jnp.where(is_tok, dgate, 0.0),
            jnp.where(is_tok, dup, 0.0),
            jnp.where(is_tok, 0.0, jnp.roll(hid, slots, axis=0)),
        ],
        axis=1,
    ).astype(bf16)

    shares = lax.dot_general(
        rows, mids, (((0,), (0,)), ((), ())), preferred_element_type=jnp.float32
    ).astype(bf16)
    parts = lax.dot_general(
        mids, weights, (((1,), (1,)), ((), ())), preferred_element_type=jnp.float32
    ).astype(bf16)
    summed = lax.psum_scatter(parts, "z", scatter_dimension=0, tiled=True)
    grads = scatter_shares(shares, 2)
    back = lax.all_to_all(
        summed.reshape(experts, own // experts, width), ("yh", "c"), split_axis=0, concat_axis=0, tiled=True
    ).reshape(own, width).astype(jnp.float32)
    high = lax.Precision.HIGHEST
    layer_out = jnp.dot(mix_out.T, back, precision=high).astype(bf16)
    grad_in = jnp.dot(pick_tok.T, back, precision=high).astype(bf16)
    grad_gate = grads[None, :, :f_dev]
    grad_up = grads[None, :, f_dev : 2 * f_dev]
    grad_down = grads[:, 2 * f_dev :].T[None]
    return (layer_out, grad_in, grad_gate, grad_up, grad_down)


def solution(mesh):
    fine = Mesh(mesh.devices.reshape(4, 4, 12, 2, 2), ("yl", "x", "z", "yh", "c"))
    dp, echip = ("yl", "x"), ("yh", "c")
    every = dp + ("z",) + echip
    return jax.shard_map(
        local,
        mesh=fine,
        in_specs=(
            P(every, None),
            P(every, None),
            P(dp, None, echip, None, None),
            P(dp, None, echip, None, None),
            P(echip, None, "z"),
            P(echip, None, "z"),
            P(echip, "z", None),
        ),
        out_specs=(
            P(every, None),
            P(every, None),
            P(echip, dp, "z"),
            P(echip, dp, "z"),
            P(echip, "z", dp),
        ),
        check_vma=False,
    )
```

```python
import jax
import jax.numpy as jnp
from jax import lax
from jax.sharding import Mesh, PartitionSpec as P


def slot_plan(expert_ids, gate_wts, experts):
    token_count, topk_count = expert_ids.shape
    entry_count = token_count * topk_count
    slots = entry_count // experts
    ids = expert_ids.reshape(entry_count)
    order = jnp.arange(entry_count)
    earlier = (ids[None, :] == ids[:, None]) & (order[None, :] < order[:, None])
    rank = jnp.sum(earlier.astype(jnp.int32), axis=1)
    row_of = ids * (2 * slots) + rank
    rows = jnp.arange(experts * 2 * slots)
    hit_tok = (rows[:, None] == row_of[None, :]).astype(jnp.float32)
    hit_cot = (rows[:, None] == (row_of + slots)[None, :]).astype(jnp.float32)
    wts = gate_wts.reshape(1, entry_count)
    pick_tok = jnp.sum(hit_tok.reshape(-1, token_count, topk_count), axis=2)
    pick_cot = jnp.sum(hit_cot.reshape(-1, token_count, topk_count), axis=2)
    mix_out = jnp.sum((hit_cot * wts).reshape(-1, token_count, topk_count), axis=2)
    cot_weight = jnp.sum(hit_cot * wts, axis=1)
    return pick_tok, pick_cot, mix_out, cot_weight, slots


def shift(value, axis, step):
    size = lax.axis_size(axis)
    return lax.ppermute(value, axis, [(i, (i + step) % size) for i in range(size)])


def total(*terms):
    return sum(term.astype(jnp.float32) for term in terms).astype(jnp.bfloat16)


def ring_gather(value, axis, ups):
    size = lax.axis_size(axis)
    blocks = {0: value}
    up = down = value
    for step in range(1, max(ups, size - 1 - ups) + 1):
        if step <= ups:
            up = shift(up, axis, 1)
            blocks[size - step] = up
        if step <= size - 1 - ups:
            down = shift(down, axis, -1)
            blocks[step] = down
    return jnp.concatenate([blocks[k] for k in range(size)], axis=0)


def ring_scatter(value, axis, ups):
    size = lax.axis_size(axis)
    rows = value.shape[0] // size
    blocks = [value[k * rows : (k + 1) * rows] for k in range(size)]
    downs = size - 1 - ups
    up, down = blocks[ups], blocks[size - downs]
    left_up, left_down = ups, downs
    while left_up or left_down:
        if left_up >= left_down:
            up = shift(up, axis, 1)
            left_up -= 1
            if left_up:
                up = total(up, blocks[left_up])
        else:
            down = shift(down, axis, -1)
            left_down -= 1
            if left_down:
                down = total(down, blocks[size - left_down])
    return total(blocks[0], up, down)


def scatter_shares(low, high):
    nx, ny = lax.axis_size("x"), lax.axis_size("yl")
    px, py = lax.axis_index("x"), lax.axis_index("yl")
    low = low.reshape(ny // 2, nx, -1, low.shape[1])
    high = high.reshape(ny // 2, nx, -1, high.shape[1])

    def chunk(step, half):
        return lax.dynamic_index_in_dim(half, (px + step) % nx, 1, keepdims=False)

    far_low = shift(chunk(2, low), "x", 1)
    far_high = shift(chunk(2, high), "x", -1)
    near_high = shift(chunk(1, high), "x", 1)
    near_low = shift(chunk(-1, low), "x", -1)
    rest_low = shift(total(chunk(1, low), far_low), "x", 1)
    rest_high = shift(total(chunk(-1, high), far_high), "x", -1)
    mine = jnp.concatenate(
        [total(chunk(0, low), near_low, rest_low), total(chunk(0, high), near_high, rest_high)], axis=0
    )

    def target(step):
        return lax.dynamic_index_in_dim(mine, (py + step) % ny, 0, keepdims=False)

    return total(target(0), *[shift(target(step), "yl", step) for step in range(1, ny)])


def local(hidden, grad_out, routes, combine, w_gate, w_up, w_down):
    experts = lax.axis_size("yh") * lax.axis_size("c")
    width = hidden.shape[1]
    half = width // 2
    f_dev = w_gate.shape[2]
    nodes = lax.axis_size("z")
    node = lax.axis_index("z")
    ids = lax.dynamic_index_in_dim(routes[0, :, 0], node, 0, keepdims=False)
    wts = lax.dynamic_index_in_dim(combine[0, :, 0], node, 0, keepdims=False)
    pick_tok, pick_cot, mix_out, cot_weight, slots = slot_plan(ids, wts, experts)
    bf16 = jnp.bfloat16
    weights = jnp.concatenate([w_gate[0], w_up[0], w_down[0].T], axis=1)

    send_tok = jnp.dot(pick_tok.astype(bf16), hidden, preferred_element_type=jnp.float32)
    send_cot = jnp.dot(pick_cot.astype(bf16), grad_out, preferred_element_type=jnp.float32)
    send = (send_tok + send_cot * cot_weight[:, None]).astype(bf16)
    own = send.shape[0]
    got = lax.all_to_all(
        send.reshape(experts, own // experts, width), ("yh", "c"), split_axis=0, concat_axis=0, tiled=True
    ).reshape(own, width)
    ups = (nodes - 1) // 2
    rows_low = ring_gather(got[:, :half], "z", ups)
    rows_high = ring_gather(got[:, half:], "z", nodes - 1 - ups)

    pre = jnp.dot(rows_low, weights[:half], preferred_element_type=jnp.float32)
    pre = pre + jnp.dot(rows_high, weights[half:], preferred_element_type=jnp.float32)
    gate_pre = pre[:, :f_dev]
    up_pre = pre[:, f_dev : 2 * f_dev]
    hidden_grad = jnp.roll(pre[:, 2 * f_dev :], -slots, axis=0)
    is_tok = ((jnp.arange(pre.shape[0]) % (2 * slots)) < slots)[:, None]
    sig = jax.nn.sigmoid(gate_pre)
    hid = gate_pre * sig * up_pre
    dgate = hidden_grad * up_pre * sig * (1.0 + gate_pre * (1.0 - sig))
    dup = hidden_grad * gate_pre * sig
    mids = jnp.concatenate(
        [
            jnp.where(is_tok, dgate, 0.0),
            jnp.where(is_tok, dup, 0.0),
            jnp.where(is_tok, 0.0, jnp.roll(hid, slots, axis=0)),
        ],
        axis=1,
    ).astype(bf16)

    def parts(block):
        return lax.dot_general(
            mids, block, (((1,), (1,)), ((), ())), preferred_element_type=jnp.float32
        ).astype(bf16)

    def shares(rows):
        return lax.dot_general(
            rows, mids, (((0,), (0,)), ((), ())), preferred_element_type=jnp.float32
        ).astype(bf16)

    summed = jnp.concatenate(
        [
            ring_scatter(parts(weights[:half]), "z", ups),
            ring_scatter(parts(weights[half:]), "z", nodes - 1 - ups),
        ],
        axis=1,
    )
    grads = scatter_shares(shares(rows_low), shares(rows_high))
    back = lax.all_to_all(
        summed.reshape(experts, own // experts, width), ("yh", "c"), split_axis=0, concat_axis=0, tiled=True
    ).reshape(own, width).astype(jnp.float32)
    high = lax.Precision.HIGHEST
    layer_out = jnp.dot(mix_out.T, back, precision=high).astype(bf16)
    grad_in = jnp.dot(pick_tok.T, back, precision=high).astype(bf16)
    grad_gate = grads[None, :, :f_dev]
    grad_up = grads[None, :, f_dev : 2 * f_dev]
    grad_down = grads[:, 2 * f_dev :].T[None]
    return (layer_out, grad_in, grad_gate, grad_up, grad_down)


def solution(mesh):
    fine = Mesh(mesh.devices.reshape(4, 4, 12, 2, 2), ("yl", "x", "z", "yh", "c"))
    dp, echip = ("yl", "x"), ("yh", "c")
    every = dp + ("z",) + echip
    return jax.shard_map(
        local,
        mesh=fine,
        in_specs=(
            P(every, None),
            P(every, None),
            P(dp, None, echip, None, None),
            P(dp, None, echip, None, None),
            P(echip, None, "z"),
            P(echip, None, "z"),
            P(echip, "z", None),
        ),
        out_specs=(
            P(every, None),
            P(every, None),
            P(echip, dp, "z"),
            P(echip, dp, "z"),
            P(echip, "z", dp),
        ),
        check_vma=False,
    )
```

```python
import jax
import jax.numpy as jnp
from jax import lax
from jax.sharding import Mesh, PartitionSpec as P


def slot_plan(expert_ids, gate_wts, experts):
    token_count, topk_count = expert_ids.shape
    entry_count = token_count * topk_count
    slots = entry_count // experts
    ids = expert_ids.reshape(entry_count)
    order = jnp.arange(entry_count)
    earlier = (ids[None, :] == ids[:, None]) & (order[None, :] < order[:, None])
    rank = jnp.sum(earlier.astype(jnp.int32), axis=1)
    row_of = ids * (2 * slots) + rank
    rows = jnp.arange(experts * 2 * slots)
    hit_tok = (rows[:, None] == row_of[None, :]).astype(jnp.float32)
    hit_cot = (rows[:, None] == (row_of + slots)[None, :]).astype(jnp.float32)
    wts = gate_wts.reshape(1, entry_count)
    pick_tok = jnp.sum(hit_tok.reshape(-1, token_count, topk_count), axis=2)
    pick_cot = jnp.sum(hit_cot.reshape(-1, token_count, topk_count), axis=2)
    mix_out = jnp.sum((hit_cot * wts).reshape(-1, token_count, topk_count), axis=2)
    cot_weight = jnp.sum(hit_cot * wts, axis=1)
    return pick_tok, pick_cot, mix_out, cot_weight, slots


def shift(value, axis, step):
    size = lax.axis_size(axis)
    return lax.ppermute(value, axis, [(i, (i + step) % size) for i in range(size)])


def total(*terms):
    return sum(term.astype(jnp.float32) for term in terms).astype(jnp.bfloat16)


def scatter_shares(shares, cuts):
    nx, ny = lax.axis_size("x"), lax.axis_size("yl")
    px, py = lax.axis_index("x"), lax.axis_index("yl")
    grid = shares.reshape(ny, nx, shares.shape[0] // (nx * ny), shares.shape[1])
    low, high = slice(0, ny // 2), slice(ny // 2, ny)
    edges = (0,) + cuts + (grid.shape[2],)
    done = []
    for piece in range(len(edges) - 1):
        part = grid[:, :, edges[piece] : edges[piece + 1]]

        def chunk(step, half):
            return lax.dynamic_index_in_dim(part[half], (px + step) % nx, 1, keepdims=False)

        right = shift(jnp.concatenate([chunk(2, low), chunk(1, high)], axis=0), "x", 1)
        left = shift(jnp.concatenate([chunk(2, high), chunk(-1, low)], axis=0), "x", -1)
        rests = lax.optimization_barrier((total(chunk(1, low), right[low]), total(chunk(-1, high), left[low])))
        rest_low = shift(rests[0], "x", 1)
        rest_high = shift(rests[1], "x", -1)
        mine = jnp.concatenate(
            [total(chunk(0, low), left[high], rest_low), total(chunk(0, high), right[high], rest_high)], axis=0
        )

        def target(step):
            return lax.dynamic_index_in_dim(mine, (py + step) % ny, 0, keepdims=False)

        others = [shift(target(step), "yl", step) for step in (2, 1, 3)]
        done.append(total(target(0), *others))
    return jnp.concatenate(done, axis=0)


def layer(hidden, grad_out, routes, combine, w_gate, w_up, w_down):
    experts = lax.axis_size("yh") * lax.axis_size("c")
    width = hidden.shape[1]
    f_dev = w_gate.shape[2]
    node = lax.axis_index("z")
    ids = lax.dynamic_index_in_dim(routes[0, :, 0], node, 0, keepdims=False)
    wts = lax.dynamic_index_in_dim(combine[0, :, 0], node, 0, keepdims=False)
    pick_tok, pick_cot, mix_out, cot_weight, slots = slot_plan(ids, wts, experts)
    bf16 = jnp.bfloat16
    weights = lax.optimization_barrier(jnp.concatenate([w_gate[0], w_up[0], w_down[0].T], axis=1))

    send_tok = jnp.dot(pick_tok.astype(bf16), hidden, preferred_element_type=jnp.float32)
    send_cot = jnp.dot(pick_cot.astype(bf16), grad_out, preferred_element_type=jnp.float32)
    send = (send_tok + send_cot * cot_weight[:, None]).astype(bf16)
    own = send.shape[0]
    wide = 3 * width // 4

    def exchange(block):
        return lax.all_to_all(
            block.reshape(experts, own // experts, block.shape[1]), ("yh", "c"), split_axis=0, concat_axis=0, tiled=True
        ).reshape(block.shape)

    rows_wide = lax.all_gather(exchange(send[:, :wide]), "z", axis=0, tiled=True)
    rows_rest = lax.all_gather(exchange(send[:, wide:]), "z", axis=0, tiled=True)

    pre = jnp.dot(rows_rest, weights[wide:], preferred_element_type=jnp.float32)
    pre = pre + jnp.dot(rows_wide, weights[:wide], preferred_element_type=jnp.float32)
    gate_pre = pre[:, :f_dev]
    up_pre = pre[:, f_dev : 2 * f_dev]
    hidden_grad = jnp.roll(pre[:, 2 * f_dev :], -slots, axis=0)
    is_tok = ((jnp.arange(pre.shape[0]) % (2 * slots)) < slots)[:, None]
    sig = jax.nn.sigmoid(gate_pre)
    hid = gate_pre * sig * up_pre
    dgate = hidden_grad * up_pre * sig * (1.0 + gate_pre * (1.0 - sig))
    dup = hidden_grad * gate_pre * sig
    mids = jnp.concatenate(
        [
            jnp.where(is_tok, dgate, 0.0),
            jnp.where(is_tok, dup, 0.0),
            jnp.where(is_tok, 0.0, jnp.roll(hid, slots, axis=0)),
        ],
        axis=1,
    ).astype(bf16)

    shares = jnp.concatenate(
        [
            lax.dot_general(
                block, mids, (((0,), (0,)), ((), ())), preferred_element_type=jnp.float32
            ).astype(bf16)
            for block in (rows_wide, rows_rest)
        ],
        axis=0,
    )
    parts = lax.dot_general(
        mids, weights, (((1,), (1,)), ((), ())), preferred_element_type=jnp.float32
    ).astype(bf16)
    summed = lax.psum_scatter(parts, "z", scatter_dimension=0, tiled=True)
    grads = scatter_shares(shares, (shares.shape[0] * 4 // (7 * 16),))
    back = exchange(summed).astype(jnp.float32)
    high = lax.Precision.HIGHEST
    layer_out = jnp.dot(mix_out.T, back, precision=high).astype(bf16)
    grad_in = jnp.dot(pick_tok.T, back, precision=high).astype(bf16)
    grad_gate = grads[None, :, :f_dev]
    grad_up = grads[None, :, f_dev : 2 * f_dev]
    grad_down = grads[:, 2 * f_dev :].T[None]
    return (layer_out, grad_in, grad_gate, grad_up, grad_down)


def solution(mesh):
    fine = Mesh(mesh.devices.reshape(4, 4, 12, 2, 2), ("yl", "x", "z", "yh", "c"))
    dp, echip = ("yl", "x"), ("yh", "c")
    every = dp + ("z",) + echip
    return jax.shard_map(
        layer,
        mesh=fine,
        in_specs=(
            P(every, None),
            P(every, None),
            P(dp, None, echip, None, None),
            P(dp, None, echip, None, None),
            P(echip, None, "z"),
            P(echip, None, "z"),
            P(echip, "z", None),
        ),
        out_specs=(
            P(every, None),
            P(every, None),
            P(echip, dp, "z"),
            P(echip, dp, "z"),
            P(echip, "z", dp),
        ),
        check_vma=False,
    )
```

```python
import jax
import jax.numpy as jnp
from jax import lax
from jax.sharding import Mesh, PartitionSpec as P


def slot_plan(expert_ids, gate_wts, experts):
    token_count, topk_count = expert_ids.shape
    entry_count = token_count * topk_count
    slots = entry_count // experts
    ids = expert_ids.reshape(entry_count)
    order = jnp.arange(entry_count)
    earlier = (ids[None, :] == ids[:, None]) & (order[None, :] < order[:, None])
    rank = jnp.sum(earlier.astype(jnp.int32), axis=1)
    row_of = ids * (2 * slots) + rank
    rows = jnp.arange(experts * 2 * slots)
    hit_tok = (rows[:, None] == row_of[None, :]).astype(jnp.float32)
    hit_cot = (rows[:, None] == (row_of + slots)[None, :]).astype(jnp.float32)
    wts = gate_wts.reshape(1, entry_count)
    pick_tok = jnp.sum(hit_tok.reshape(-1, token_count, topk_count), axis=2)
    pick_cot = jnp.sum(hit_cot.reshape(-1, token_count, topk_count), axis=2)
    mix_out = jnp.sum((hit_cot * wts).reshape(-1, token_count, topk_count), axis=2)
    cot_weight = jnp.sum(hit_cot * wts, axis=1)
    return pick_tok, pick_cot, mix_out, cot_weight, slots


def shift(value, axis, step):
    size = lax.axis_size(axis)
    return lax.ppermute(value, axis, [(i, (i + step) % size) for i in range(size)])


def total(*terms):
    return sum(term.astype(jnp.float32) for term in terms).astype(jnp.bfloat16)


def scatter_shares(shares, cuts):
    nx, ny = lax.axis_size("x"), lax.axis_size("yl")
    px, py = lax.axis_index("x"), lax.axis_index("yl")
    grid = shares.reshape(ny, nx, shares.shape[0] // (nx * ny), shares.shape[1])
    low, high = slice(0, ny // 2), slice(ny // 2, ny)
    edges = (0,) + cuts + (grid.shape[2],)
    done = []
    for piece in range(len(edges) - 1):
        part = grid[:, :, edges[piece] : edges[piece + 1]]

        def chunk(step, half):
            return lax.dynamic_index_in_dim(part[half], (px + step) % nx, 1, keepdims=False)

        right = shift(jnp.concatenate([chunk(2, low), chunk(1, high)], axis=0), "x", 1)
        left = shift(jnp.concatenate([chunk(2, high), chunk(-1, low)], axis=0), "x", -1)
        rests = lax.optimization_barrier((total(chunk(1, low), right[low]), total(chunk(-1, high), left[low])))
        rest_low = shift(rests[0], "x", 1)
        rest_high = shift(rests[1], "x", -1)
        mine = jnp.concatenate(
            [total(chunk(0, low), left[high], rest_low), total(chunk(0, high), right[high], rest_high)], axis=0
        )

        def target(step):
            return lax.dynamic_index_in_dim(mine, (py + step) % ny, 0, keepdims=False)

        others = [shift(target(step), "yl", step) for step in (2, 1, 3)]
        done.append(total(target(0), *others))
    return jnp.concatenate(done, axis=0)


def layer(hidden, grad_out, routes, combine, w_gate, w_up, w_down):
    experts = lax.axis_size("yh") * lax.axis_size("c")
    width = hidden.shape[1]
    f_dev = w_gate.shape[2]
    node = lax.axis_index("z")
    ids = lax.dynamic_index_in_dim(routes[0, :, 0], node, 0, keepdims=False)
    wts = lax.dynamic_index_in_dim(combine[0, :, 0], node, 0, keepdims=False)
    pick_tok, pick_cot, mix_out, cot_weight, slots = slot_plan(ids, wts, experts)
    bf16 = jnp.bfloat16
    weights = lax.optimization_barrier(jnp.concatenate([w_gate[0], w_up[0], w_down[0].T], axis=1))

    send_tok = jnp.dot(pick_tok.astype(bf16), hidden, preferred_element_type=jnp.float32)
    send_cot = jnp.dot(pick_cot.astype(bf16), grad_out, preferred_element_type=jnp.float32)
    send = (send_tok + send_cot * cot_weight[:, None]).astype(bf16)
    own = send.shape[0]
    got = lax.all_to_all(
        send.reshape(experts, own // experts, width), ("yh", "c"), split_axis=0, concat_axis=0, tiled=True
    ).reshape(own, width)
    rows = lax.all_gather(got, "z", axis=0, tiled=True)

    pre = jnp.dot(rows, weights, preferred_element_type=jnp.float32)
    gate_pre = pre[:, :f_dev]
    up_pre = pre[:, f_dev : 2 * f_dev]
    hidden_grad = jnp.roll(pre[:, 2 * f_dev :], -slots, axis=0)
    is_tok = ((jnp.arange(rows.shape[0]) % (2 * slots)) < slots)[:, None]
    sig = jax.nn.sigmoid(gate_pre)
    hid = gate_pre * sig * up_pre
    dgate = hidden_grad * up_pre * sig * (1.0 + gate_pre * (1.0 - sig))
    dup = hidden_grad * gate_pre * sig
    mids = jnp.concatenate(
        [
            jnp.where(is_tok, dgate, 0.0),
            jnp.where(is_tok, dup, 0.0),
            jnp.where(is_tok, 0.0, jnp.roll(hid, slots, axis=0)),
        ],
        axis=1,
    ).astype(bf16)

    shares = lax.dot_general(
        rows, mids, (((0,), (0,)), ((), ())), preferred_element_type=jnp.float32
    ).astype(bf16)
    parts = lax.dot_general(
        mids, weights, (((1,), (1,)), ((), ())), preferred_element_type=jnp.float32
    ).astype(bf16)
    summed = lax.psum_scatter(parts, "z", scatter_dimension=0, tiled=True)
    grads = scatter_shares(shares, (144,))
    back = lax.all_to_all(
        summed.reshape(experts, own // experts, width), ("yh", "c"), split_axis=0, concat_axis=0, tiled=True
    ).reshape(own, width).astype(jnp.float32)
    high = lax.Precision.HIGHEST
    layer_out = jnp.dot(mix_out.T, back, precision=high).astype(bf16)
    grad_in = jnp.dot(pick_tok.T, back, precision=high).astype(bf16)
    grad_gate = grads[None, :, :f_dev]
    grad_up = grads[None, :, f_dev : 2 * f_dev]
    grad_down = grads[:, 2 * f_dev :].T[None]
    return (layer_out, grad_in, grad_gate, grad_up, grad_down)


def solution(mesh):
    fine = Mesh(mesh.devices.reshape(4, 4, 12, 2, 2), ("yl", "x", "z", "yh", "c"))
    dp, echip = ("yl", "x"), ("yh", "c")
    every = dp + ("z",) + echip
    return jax.shard_map(
        layer,
        mesh=fine,
        in_specs=(
            P(every, None),
            P(every, None),
            P(dp, None, echip, None, None),
            P(dp, None, echip, None, None),
            P(echip, None, "z"),
            P(echip, None, "z"),
            P(echip, "z", None),
        ),
        out_specs=(
            P(every, None),
            P(every, None),
            P(echip, dp, "z"),
            P(echip, dp, "z"),
            P(echip, "z", dp),
        ),
        check_vma=False,
    )
```

```python
import jax
import jax.numpy as jnp
from jax import lax
from jax.sharding import Mesh, PartitionSpec as P


def slot_plan(expert_ids, gate_wts, experts):
    token_count, topk_count = expert_ids.shape
    entry_count = token_count * topk_count
    slots = entry_count // experts
    ids = expert_ids.reshape(entry_count)
    order = jnp.arange(entry_count)
    earlier = (ids[None, :] == ids[:, None]) & (order[None, :] < order[:, None])
    rank = jnp.sum(earlier.astype(jnp.int32), axis=1)
    row_of = ids * (2 * slots) + rank
    rows = jnp.arange(experts * 2 * slots)
    hit_tok = (rows[:, None] == row_of[None, :]).astype(jnp.float32)
    hit_cot = (rows[:, None] == (row_of + slots)[None, :]).astype(jnp.float32)
    wts = gate_wts.reshape(1, entry_count)
    pick_tok = jnp.sum(hit_tok.reshape(-1, token_count, topk_count), axis=2)
    pick_cot = jnp.sum(hit_cot.reshape(-1, token_count, topk_count), axis=2)
    mix_out = jnp.sum((hit_cot * wts).reshape(-1, token_count, topk_count), axis=2)
    cot_weight = jnp.sum(hit_cot * wts, axis=1)
    return pick_tok, pick_cot, mix_out, cot_weight, slots


def shift(value, axis, step):
    size = lax.axis_size(axis)
    return lax.ppermute(value, axis, [(i, (i + step) % size) for i in range(size)])


def total(*terms):
    return sum(term.astype(jnp.float32) for term in terms).astype(jnp.bfloat16)


def scatter_shares(shares, pieces):
    nx, ny = lax.axis_size("x"), lax.axis_size("yl")
    px, py = lax.axis_index("x"), lax.axis_index("yl")
    grid = shares.reshape(ny, nx, shares.shape[0] // (nx * ny), shares.shape[1])
    rows = grid.shape[2] // pieces
    low, high = slice(0, ny // 2), slice(ny // 2, ny)
    done = []
    for piece in range(pieces):
        part = grid[:, :, piece * rows : (piece + 1) * rows]

        def chunk(step, half):
            return lax.dynamic_index_in_dim(part[half], (px + step) % nx, 1, keepdims=False)

        far_low = shift(chunk(2, low), "x", 1)
        far_high = shift(chunk(2, high), "x", -1)
        near_high = shift(chunk(1, high), "x", 1)
        near_low = shift(chunk(-1, low), "x", -1)
        rest_low = shift(total(chunk(1, low), far_low), "x", 1)
        rest_high = shift(total(chunk(-1, high), far_high), "x", -1)
        mine = jnp.concatenate(
            [total(chunk(0, low), near_low, rest_low), total(chunk(0, high), near_high, rest_high)], axis=0
        )

        def target(step):
            return lax.dynamic_index_in_dim(mine, (py + step) % ny, 0, keepdims=False)

        others = [shift(target(step), "yl", step) for step in range(1, ny)]
        done.append(total(target(0), *others))
    return jnp.concatenate(done, axis=0)


def layer(hidden, grad_out, routes, combine, w_gate, w_up, w_down):
    experts = lax.axis_size("yh") * lax.axis_size("c")
    width = hidden.shape[1]
    f_dev = w_gate.shape[2]
    node = lax.axis_index("z")
    ids = lax.dynamic_index_in_dim(routes[0, :, 0], node, 0, keepdims=False)
    wts = lax.dynamic_index_in_dim(combine[0, :, 0], node, 0, keepdims=False)
    pick_tok, pick_cot, mix_out, cot_weight, slots = slot_plan(ids, wts, experts)
    bf16 = jnp.bfloat16
    weights = jnp.concatenate([w_gate[0], w_up[0], w_down[0].T], axis=1)

    send_tok = jnp.dot(pick_tok.astype(bf16), hidden, preferred_element_type=jnp.float32)
    send_cot = jnp.dot(pick_cot.astype(bf16), grad_out, preferred_element_type=jnp.float32)
    send = (send_tok + send_cot * cot_weight[:, None]).astype(bf16)
    own = send.shape[0]
    got = lax.all_to_all(
        send.reshape(experts, own // experts, width), ("yh", "c"), split_axis=0, concat_axis=0, tiled=True
    ).reshape(own, width)
    rows = lax.all_gather(got, "z", axis=0, tiled=True)

    pre = jnp.dot(rows, weights, preferred_element_type=jnp.float32)
    gate_pre = pre[:, :f_dev]
    up_pre = pre[:, f_dev : 2 * f_dev]
    hidden_grad = jnp.roll(pre[:, 2 * f_dev :], -slots, axis=0)
    is_tok = ((jnp.arange(rows.shape[0]) % (2 * slots)) < slots)[:, None]
    sig = jax.nn.sigmoid(gate_pre)
    hid = gate_pre * sig * up_pre
    dgate = hidden_grad * up_pre * sig * (1.0 + gate_pre * (1.0 - sig))
    dup = hidden_grad * gate_pre * sig
    mids = jnp.concatenate(
        [
            jnp.where(is_tok, dgate, 0.0),
            jnp.where(is_tok, dup, 0.0),
            jnp.where(is_tok, 0.0, jnp.roll(hid, slots, axis=0)),
        ],
        axis=1,
    ).astype(bf16)

    shares = lax.dot_general(
        rows, mids, (((0,), (0,)), ((), ())), preferred_element_type=jnp.float32
    ).astype(bf16)
    parts = lax.dot_general(
        mids, weights, (((1,), (1,)), ((), ())), preferred_element_type=jnp.float32
    ).astype(bf16)
    summed = lax.psum_scatter(parts, "z", scatter_dimension=0, tiled=True)
    grads = scatter_shares(shares, 2)
    back = lax.all_to_all(
        summed.reshape(experts, own // experts, width), ("yh", "c"), split_axis=0, concat_axis=0, tiled=True
    )
    back = back.reshape(own, width).astype(jnp.float32)
    high = lax.Precision.HIGHEST
    layer_out = jnp.dot(mix_out.T, back, precision=high).astype(bf16)
    grad_in = jnp.dot(pick_tok.T, back, precision=high).astype(bf16)
    grad_gate = grads[None, :, :f_dev]
    grad_up = grads[None, :, f_dev : 2 * f_dev]
    grad_down = grads[:, 2 * f_dev :].T[None]
    return (layer_out, grad_in, grad_gate, grad_up, grad_down)


def solution(mesh):
    fine = Mesh(mesh.devices.reshape(4, 4, 12, 2, 2), ("yl", "x", "z", "yh", "c"))
    dp, echip = ("yl", "x"), ("yh", "c")
    every = dp + ("z",) + echip
    return jax.shard_map(
        layer,
        mesh=fine,
        in_specs=(
            P(every, None),
            P(every, None),
            P(dp, None, echip, None, None),
            P(dp, None, echip, None, None),
            P(echip, None, "z"),
            P(echip, None, "z"),
            P(echip, "z", None),
        ),
        out_specs=(
            P(every, None),
            P(every, None),
            P(echip, dp, "z"),
            P(echip, dp, "z"),
            P(echip, "z", dp),
        ),
        check_vma=False,
    )
```
